32 devices in a mesh: groups: 2 (over y), seq: 4 (over z), mp: 2 (over x), branch: 2 (over core).
Axes of the slice: x: 2, y: 2, z: 4, core: 2. Of those that a mesh axis runs over, the one named last changes fastest.
Arguments:
- streams: float32 [2, 8, 256, 1152], P('branch', ('groups', 'seq')), parts along dimension 1, may hold values from -6 to 6
- modulation: float32 [2, 6, 1152], P('branch'), may hold values from -3 to 3
- s_qkv: bfloat16 [2, 1152, 3, 1152], P('branch', 'seq', None, 'mp'), may hold values from -0.1875 to 0.1875
- s_out: bfloat16 [2, 1152, 1152], P('branch', 'mp', 'seq'), may hold values from -0.25 to 0.25
- w_in: bfloat16 [2, 1152, 4608], P('branch', 'seq', 'mp'), may hold values from -0.1875 to 0.1875
- w_out: bfloat16 [2, 4608, 1152], P('branch', 'mp', 'seq'), may hold values from -0.125 to 0.125
- hint_gain: float32 [13, 1152], replicated, may hold values from 0.3 to 3
- inject_layer: int32 [4], replicated, may hold values from 0 to 12
- hint_weight: bfloat16 [1152, 1152], P('seq', 'mp'), may hold values from -0.1875 to 0.1875
- t_mod: float32 [3, 1152], replicated, may hold values from -3 to 3
- t_qkv: bfloat16 [1152, 3, 1152], P('seq', None, 'mp'), may hold values from -0.1875 to 0.1875
- t_out: bfloat16 [1152, 1152], P('mp', 'seq'), may hold values from -0.25 to 0.25
Outputs:
- main_out: float32 [8, 256, 1152], P('groups', ('seq', 'branch'), 'mp'), parts along dimension 0
The draws below stay inside these ranges and needn't reach their ends.
There are 2 independent parts, one for each index of `groups`. The reference program is written for one: setup_inputs(seed, part) draws one part's arguments, and reference() takes and returns one part's arrays. A program takes and returns all parts, laid end to end along the dimension named above; an argument that names none is the same for every part. Nothing has to cross between parts.
All inputs are finite; a program needn't handle non-finite values.
Results may differ from the reference program's by a relative error of at most 0.014.
Values may be sent and summed in bfloat16 or wider, within the bound.
No kernel may reach another device: no remote copies, remote signals or barrier semaphores. Data moves between devices by JAX's collectives and lax.ppermute only.
A program may use at most 64 MiB of HBM per device.

```python
import math
import jax
import jax.numpy as jnp
from jax import lax

D = 1152
FF = 4608
HEADS = 16
HEAD_DIM = 72
HINT_LAYERS = 13
TPF = 256
FRAMES = 4


def touch_ends(values, key, least, top_value):
    dims = values.shape
    index_at = [jax.random.randint(jax.random.fold_in(key, axis), (), 0, dims[axis]) for axis in range(len(dims))]
    values = values.at[tuple(index_at)].set(least)
    longest = dims.index(max(dims))
    index_at[longest] = (index_at[longest] + 1) % dims[longest]
    return values.at[tuple(index_at)].set(top_value)


def spiked(drawn, stream_key, source, target, shards_of, factor):
    def block_of(axis_at):
        return (jnp.arange(drawn.shape[axis_at]) // (drawn.shape[axis_at] // shards_of)).reshape((-1,) + (1,) * (drawn.ndim - 1 - axis_at))

    first = jax.random.permutation(stream_key, shards_of)[block_of(target)]
    second = (block_of(target) + shards_of // 2) % shards_of
    return jnp.where((block_of(source) == first) | (block_of(source) == second), factor * drawn, drawn)


def steps_of(stream_key, extent, pieces, low, high):
    level = 1.0
    for axis_at, parts in pieces:
        heights = jax.random.uniform(jax.random.fold_in(jax.random.fold_in(stream_key, 6), axis_at), (parts,), jnp.float32, low / len(pieces), high / len(pieces))
        level = level * jnp.repeat(jnp.exp(heights), extent[axis_at] // parts).reshape((-1,) + (1,) * (len(extent) - 1 - axis_at))
    return level


def bell_draw(rng, shape, spread, reach, pieces=(), kind=jnp.bfloat16):
    array = jax.random.normal(rng, shape, jnp.float32) * spread
    if len(pieces) > 0:
        array = steps_of(rng, shape, pieces, -0.22, 0.18) * array
    return jnp.clip(array, min=-reach, max=reach).astype(kind)


def bell_draw_with(key, shape, deviation, limit, split, heavy, held_as=jnp.bfloat16):
    values = deviation * jax.random.normal(key, shape, jnp.float32)
    if split:
        values = values * steps_of(key, shape, split, -0.22, 0.18)
    return jnp.clip(spiked(values, jax.random.fold_in(key, 3), *heavy), -limit, limit).astype(held_as)


def setup_inputs(seed: int = 0, part: int = 0) -> dict:
    splits = jax.random.split(jax.random.key(seed), 13)
    part_keys = jax.random.split(jax.random.fold_in(splits[12], part), 13)
    return {
        "streams": bell_draw(part_keys[0], (2, FRAMES, TPF, D), 1.0, 6.0, ((0, 2), (1, 4)), jnp.float32),
        "modulation": bell_draw(splits[1], (2, 6, D), 0.7, 3.0, ((0, 2),), jnp.float32),
        "s_qkv": bell_draw(splits[2], (2, D, 3, D), D ** -0.5, 0.1875, ((0, 2), (1, 4), (3, 2))),
        "s_out": bell_draw_with(splits[3], (2, D, D), D ** -0.5, 0.25, ((0, 2), (1, 2), (2, 4)), (1, 2, 4, 2.0)),
        "w_in": bell_draw(splits[4], (2, D, FF), D ** -0.5, 0.1875, ((0, 2), (1, 4), (2, 2))),
        "w_out": bell_draw_with(splits[5], (2, FF, D), FF ** -0.5, 0.125, ((0, 2), (1, 2), (2, 4)), (1, 2, 4, 2.0)),
        "hint_gain": jnp.clip(jnp.exp(jax.random.uniform(splits[6], (HINT_LAYERS, D), jnp.float32, math.log(0.3), math.log(3.0))), 0.3, 3.0),
        "inject_layer": touch_ends(jax.random.randint(splits[7], (FRAMES,), 0, HINT_LAYERS), jax.random.fold_in(splits[7], 1), 0, HINT_LAYERS - 1).astype(jnp.int32),
        "hint_weight": bell_draw(splits[8], (D, D), D ** -0.5, 0.1875, ((0, 4), (1, 2))),
        "t_mod": bell_draw(splits[9], (3, D), 0.7, 3.0, (), jnp.float32),
        "t_qkv": bell_draw(splits[10], (D, 3, D), D ** -0.5, 0.1875, ((0, 4), (2, 2))),
        "t_out": bell_draw_with(splits[11], (D, D), D ** -0.5, 0.25, ((0, 2), (1, 4)), (0, 1, 4, 2.0)),
    }


def layer_norm(value, shift, scale):
    mean = lax.optimization_barrier(jnp.mean(value, axis=-1, keepdims=True))
    centred = value - mean
    var = lax.optimization_barrier(jnp.mean(centred * centred, axis=-1, keepdims=True))
    return centred * lax.rsqrt(var + 1e-06) * (1.0 + scale) + shift

def attend(query, keys, values):
    scores = jnp.einsum('qhd,khd->hqk', query, keys, precision=lax.Precision.HIGHEST) / jnp.sqrt(jnp.float32(HEAD_DIM))
    weights = jnp.exp(scores)
    weights = weights / lax.optimization_barrier(jnp.sum(weights, axis=-1, keepdims=True))
    result = jnp.einsum('hqk,khd->qhd', weights, values, precision=lax.Precision.HIGHEST)
    return result.reshape(result.shape[0], -1)

def spatial_block(stream, mods, qkv_w, out_w, in_w, down_w):
    normed = layer_norm(stream, mods[0], mods[1]).astype(jnp.bfloat16)
    qkv = jnp.dot(normed, qkv_w.reshape(D, 3 * D), preferred_element_type=jnp.float32)
    qkv = qkv.reshape(TPF, 3, HEADS, HEAD_DIM)
    attended = attend(qkv[:, 0], qkv[:, 1], qkv[:, 2]).astype(jnp.bfloat16)
    stream = stream + mods[2] * jnp.dot(attended, out_w, preferred_element_type=jnp.float32)
    normed = layer_norm(stream, mods[3], mods[4]).astype(jnp.bfloat16)
    hidden = jax.nn.gelu(jnp.dot(normed, in_w, preferred_element_type=jnp.float32), approximate=True).astype(jnp.bfloat16)
    return stream + mods[5] * jnp.dot(hidden, down_w, preferred_element_type=jnp.float32)

def reference(streams, modulation, s_qkv, s_out, w_in, w_out, hint_gain, inject_layer, hint_weight, t_mod, t_qkv, t_out):
    outputs = []
    for section in range(2):

        def one_frame(frame, section=section):
            return spatial_block(frame, modulation[section], s_qkv[section], s_out[section], w_in[section], w_out[section])
        outputs.append(lax.map(one_frame, streams[section]))
    control, main = (outputs[0], outputs[1])
    picks = (inject_layer[:, None] == jnp.arange(HINT_LAYERS, dtype=jnp.int32)[None, :]).astype(jnp.float32)
    gain = lax.optimization_barrier(jnp.sum(picks[:, :, None] * hint_gain[None, :, :], axis=1))
    hint_in = (control * gain[:, None, :]).astype(jnp.bfloat16).reshape(FRAMES * TPF, D)
    joined = main.reshape(FRAMES * TPF, D) + jnp.dot(hint_in, hint_weight, preferred_element_type=jnp.float32)
    normed = layer_norm(joined, t_mod[0], t_mod[1]).astype(jnp.bfloat16)
    tqkv = jnp.dot(normed, t_qkv.reshape(D, 3 * D), preferred_element_type=jnp.float32)
    tqkv = tqkv.reshape(FRAMES, TPF, 3, HEADS, HEAD_DIM).transpose(1, 0, 2, 3, 4)
    attended = jax.vmap(attend)(tqkv[:, :, 0], tqkv[:, :, 1], tqkv[:, :, 2])
    attended = attended.transpose(1, 0, 2).reshape(FRAMES * TPF, D).astype(jnp.bfloat16)
    result = joined + t_mod[2] * jnp.dot(attended, t_out, preferred_element_type=jnp.float32)
    return result.reshape(FRAMES, TPF, D)
```

```python
import functools
import math

import jax
import jax.numpy as jnp
from jax import lax
from jax.experimental import pallas as pl
from jax.experimental.pallas import tpu as pltpu
from jax.sharding import PartitionSpec as P

HEAD_DIM = 72
BF16 = jnp.bfloat16
F32 = jnp.float32
NT = (((1,), (1,)), ((), ()))
VMEM_LIMIT = 48 * 1024 * 1024


def layer_norm(value, shift, scale):
    mean = jnp.mean(value, axis=-1, keepdims=True)
    centred = value - mean
    var = jnp.mean(centred * centred, axis=-1, keepdims=True)
    return centred * lax.rsqrt(var + 1e-06) * (1.0 + scale) + shift


def head_of(shape, axis):
    return lax.broadcasted_iota(jnp.int32, shape, axis) // HEAD_DIM


def spatial_kernel(lanes, h_ref, w_ref, out_ref):
    qkv = jnp.dot(h_ref[0], w_ref[...], preferred_element_type=F32)
    tokens = qkv.shape[0]
    query = qkv[:, :lanes]
    keys = qkv[:, lanes : 2 * lanes].astype(BF16)
    values = qkv[:, 2 * lanes : 3 * lanes].astype(BF16)
    heads = lanes // HEAD_DIM
    at = jnp.zeros((tokens, lanes), F32)
    owner = head_of((tokens, lanes), 1)
    for head in range(heads):
        mine = owner == head
        scores = lax.dot_general(
            jnp.where(mine, query, 0.0).astype(BF16), keys, NT, preferred_element_type=F32
        )
        weights = jnp.exp(scores / math.sqrt(HEAD_DIM))
        total = jnp.sum(weights, axis=-1, keepdims=True)
        mixed = jnp.dot(weights.astype(BF16), values, preferred_element_type=F32)
        at = jnp.where(mine, mixed / total, at)
    padded = jnp.concatenate([jnp.zeros((tokens, 3 * lanes), F32), at], axis=1).astype(BF16)
    out_ref[0] = lax.dot_general(padded, w_ref[...], NT, preferred_element_type=F32)


def spatial_attention(h, packed):
    frames, tokens, width = h.shape
    lanes = packed.shape[1] // 4
    return pl.pallas_call(
        functools.partial(spatial_kernel, lanes),
        grid=(frames,),
        in_specs=[
            pl.BlockSpec((1, tokens, width), lambda i: (i, 0, 0)),
            pl.BlockSpec(packed.shape, lambda i: (0, 0)),
        ],
        out_specs=pl.BlockSpec((1, tokens, width), lambda i: (i, 0, 0)),
        out_shape=jax.ShapeDtypeStruct((frames, tokens, width), F32),
        compiler_params=pltpu.CompilerParams(vmem_limit_bytes=VMEM_LIMIT),
        cost_estimate=pl.CostEstimate(
            flops=8 * frames * tokens * width * width, bytes_accessed=2 * width * width, transcendentals=0
        ),
    )(h, packed)


def temporal_kernel(lanes, frames, j_ref, w_ref, mod_ref, out_ref):
    ht = layer_norm(j_ref[...].astype(F32), mod_ref[0:1], mod_ref[1:2]).astype(BF16)
    rows = ht.shape[0] // frames
    qkv = jnp.dot(ht, w_ref[...], preferred_element_type=F32).reshape(frames, rows, 4 * lanes)
    query, keys = qkv[:, :, :lanes], qkv[:, :, lanes : 2 * lanes]
    values = qkv[:, :, 2 * lanes : 3 * lanes]
    pairs = (query[:, None] * keys[None]).reshape(frames * frames * rows, lanes)
    gather = (head_of((lanes, 128), 0) == lax.broadcasted_iota(jnp.int32, (lanes, 128), 1)).astype(F32)
    spread = (head_of((128, lanes), 1) == lax.broadcasted_iota(jnp.int32, (128, lanes), 0)).astype(F32)
    scores = jnp.dot(pairs, gather, precision=lax.Precision.HIGHEST, preferred_element_type=F32)
    weights = jnp.exp(scores / math.sqrt(HEAD_DIM)).reshape(frames, frames, rows, 128)
    weights = weights / jnp.sum(weights, axis=1, keepdims=True)
    wide = jnp.dot(
        weights.reshape(frames * frames * rows, 128).astype(BF16),
        spread.astype(BF16),
        preferred_element_type=F32,
    ).reshape(frames, frames, rows, lanes)
    at = jnp.sum(wide * values[None], axis=1).reshape(frames * rows, lanes)
    padded = jnp.concatenate([jnp.zeros((frames * rows, 3 * lanes), F32), at], axis=1).astype(BF16)
    out_ref[...] = lax.dot_general(padded, w_ref[...], NT, preferred_element_type=F32)


def temporal_attention(joined, packed, t_mod, frames):
    rows, width = joined.shape
    return pl.pallas_call(
        functools.partial(temporal_kernel, packed.shape[1] // 4, frames),
        out_shape=jax.ShapeDtypeStruct((rows, width), F32),
        compiler_params=pltpu.CompilerParams(vmem_limit_bytes=VMEM_LIMIT),
        cost_estimate=pl.CostEstimate(
            flops=4 * rows * width * width, bytes_accessed=2 * width * width, transcendentals=0
        ),
    )(joined, packed, t_mod)


def on_device(
    sizes,
    streams,
    modulation,
    s_qkv,
    s_out,
    w_in,
    w_out,
    hint_gain,
    inject_layer,
    hint_weight,
    t_mod,
    t_qkv,
    t_out,
):
    n_groups, n_seq, n_mp, n_branch = (sizes[a] for a in ("groups", "seq", "mp", "branch"))
    group, plane, part, core = (lax.axis_index(a) for a in ("groups", "seq", "mp", "branch"))
    x, mods = streams[0, 0], modulation[0]
    tokens, width = x.shape
    spots = tokens // (n_seq * n_branch * n_mp)
    own_tokens = tokens // n_mp

    def pick(array, index, count, axis):
        size = array.shape[axis] // count
        picked = lax.slice_in_dim(array, 0, size, axis=axis)
        for i in range(1, count):
            picked = jnp.where(index == i, lax.slice_in_dim(array, i * size, (i + 1) * size, axis=axis), picked)
        return picked

    def hop(value, by_group, by_part):
        if by_group % n_groups == 0 and by_part % n_mp == 0:
            return value
        pairs = [
            (g * n_mp + m, (g + by_group) % n_groups * n_mp + (m + by_part) % n_mp)
            for g in range(n_groups)
            for m in range(n_mp)
        ]
        return lax.ppermute(value, ("groups", "mp"), pairs)

    spread = [(g, m) for g in range(n_groups) for m in range(n_mp)]

    def gather(piece):
        return lax.all_gather(piece, "seq", axis=0, tiled=True)

    def pack(qkv, out):
        cols = pick(qkv, group, n_groups, 2)
        return jnp.concatenate([cols[:, 0], cols[:, 1], cols[:, 2], pick(out, group, n_groups, 0).T], axis=1)

    s_packed = gather(pack(s_qkv[0], s_out[0]))
    up_w = gather(pick(w_in[0], group, n_groups, 1))
    down_w = gather(pick(w_out[0], group, n_groups, 0).T)

    def both_cores(piece):
        halves = lax.all_gather(gather(piece[None]), "branch", axis=1)
        return halves.reshape(n_seq * n_branch * piece.shape[0], piece.shape[1])

    hint_half = both_cores(pick(hint_weight, core, n_branch, 0))
    t_packed = both_cores(pick(pack(t_qkv, t_out), core, n_branch, 0))
    hint_w = lax.all_gather(hint_half, "mp", axis=1, tiled=True)

    blocks = x.reshape(n_seq * n_branch, n_mp, spots, width)
    x = jnp.concatenate(
        [
            lax.dynamic_index_in_dim(blocks, (part + i) % n_mp, 1, False).reshape(own_tokens, width)
            for i in range(n_mp)
        ],
        axis=0,
    )
    h = layer_norm(x, mods[0], mods[1]).astype(BF16)
    h = jnp.stack([hop(h, -g, 0) for g in range(n_groups)])
    partial_out = spatial_attention(h, s_packed).reshape(n_groups, n_mp, own_tokens, width)

    def sum_at_owner(values):
        total = values[0, 0].astype(F32)
        for g, m in spread[1:]:
            total = total + hop(values[g, m].astype(BF16), g, m).astype(F32)
        return total

    x1 = x[:own_tokens] + mods[2] * sum_at_owner({k: partial_out[k] for k in spread})
    h2 = layer_norm(x1, mods[3], mods[4]).astype(BF16)
    rows = jnp.concatenate([hop(h2, -g, -m) for g, m in spread], axis=0)
    hidden = jax.nn.gelu(jnp.dot(rows, up_w, preferred_element_type=F32), approximate=True).astype(BF16)
    hidden = lax.optimization_barrier(hidden)
    down = lax.dot_general(hidden, down_w, NT, preferred_element_type=F32)
    down = down.reshape(len(spread), own_tokens, width)
    y = x1 + mods[5] * sum_at_owner({k: down[i] for i, k in enumerate(spread)})

    moved = lax.all_to_all(
        y.astype(BF16).reshape(1, n_seq, n_branch, spots, width), "branch", split_axis=2, concat_axis=0, tiled=True
    ).reshape(2, n_seq * spots, width)
    layer = lax.dynamic_index_in_dim(inject_layer, plane, 0, False)
    gain = lax.dynamic_index_in_dim(hint_gain, layer, 0, False)
    hint_in = (moved[0].astype(F32) * gain).astype(BF16)
    joined = moved[1].astype(F32) + jnp.dot(hint_in, hint_w, preferred_element_type=F32)

    joined = lax.all_to_all(
        joined.astype(BF16).reshape(n_seq, spots, width), "seq", split_axis=0, concat_axis=0, tiled=True
    )
    around = jnp.stack([hop(joined, -g, -m) for g, m in spread]).reshape(n_groups, n_mp, n_seq, spots, width)
    order = [(i - part + n_mp) % n_mp for i in range(n_mp)]
    around = jnp.stack([lax.dynamic_index_in_dim(around, i, 1, False) for i in order], axis=1)
    at_in = around.transpose(2, 0, 1, 3, 4)
    partial_t = temporal_attention(at_in.reshape(-1, width), t_packed, t_mod, n_seq)
    partial_t = partial_t.reshape(n_seq, n_groups, n_mp * spots, n_mp, width // n_mp)
    sends = {
        (g, m): lax.dynamic_index_in_dim(partial_t[:, g], (part + m) % n_mp, 2, False)
        for g, m in spread
    }
    result = sum_at_owner(sends)
    mine = around[0].transpose(1, 0, 2, 3).reshape(n_seq, n_mp * spots, n_mp, width // n_mp)
    mine = lax.dynamic_index_in_dim(mine, part, 2, False).astype(F32)
    gate = lax.dynamic_index_in_dim(t_mod[2].reshape(n_mp, width // n_mp), part, 0, False)
    return mine + gate * result


def solution(mesh):
    in_specs = (
        P("branch", ("groups", "seq"), None, None),
        P("branch", None, None),
        P("branch", "seq", None, "mp"),
        P("branch", "mp", "seq"),
        P("branch", "seq", "mp"),
        P("branch", "mp", "seq"),
        P(),
        P(),
        P("seq", "mp"),
        P(),
        P("seq", None, "mp"),
        P("mp", "seq"),
    )
    out_specs = P("groups", ("seq", "branch"), "mp")
    return jax.shard_map(
        functools.partial(on_device, dict(mesh.shape)),
        mesh=mesh,
        in_specs=in_specs,
        out_specs=out_specs,
        check_vma=False,
    )
```

```python
import functools
import math

import jax
import jax.numpy as jnp
from jax import lax
from jax.experimental import pallas as pl
from jax.experimental.pallas import tpu as pltpu
from jax.sharding import PartitionSpec as P

HEAD_DIM = 72
BF16 = jnp.bfloat16
F32 = jnp.float32
NT = (((1,), (1,)), ((), ()))
VMEM_LIMIT = 48 * 1024 * 1024


def layer_norm(value, shift, scale):
    mean = jnp.mean(value, axis=-1, keepdims=True)
    centred = value - mean
    var = jnp.mean(centred * centred, axis=-1, keepdims=True)
    return centred * lax.rsqrt(var + 1e-06) * (1.0 + scale) + shift


def head_of(shape, axis):
    return lax.broadcasted_iota(jnp.int32, shape, axis) // HEAD_DIM


def spatial_kernel(lanes, h_ref, w_ref, out_ref):
    qkv = jnp.dot(h_ref[0], w_ref[...], preferred_element_type=F32)
    tokens = qkv.shape[0]
    query = qkv[:, :lanes]
    keys = qkv[:, lanes : 2 * lanes].astype(BF16)
    values = qkv[:, 2 * lanes : 3 * lanes].astype(BF16)
    heads = lanes // HEAD_DIM
    at = jnp.zeros((tokens, lanes), F32)
    owner = head_of((tokens, lanes), 1)
    for head in range(heads):
        mine = owner == head
        scores = lax.dot_general(
            jnp.where(mine, query, 0.0).astype(BF16), keys, NT, preferred_element_type=F32
        )
        weights = jnp.exp(scores / math.sqrt(HEAD_DIM))
        total = jnp.sum(weights, axis=-1, keepdims=True)
        mixed = jnp.dot(weights.astype(BF16), values, preferred_element_type=F32)
        at = jnp.where(mine, mixed / total, at)
    padded = jnp.concatenate([jnp.zeros((tokens, 3 * lanes), F32), at], axis=1).astype(BF16)
    out_ref[0] = lax.dot_general(padded, w_ref[...], NT, preferred_element_type=F32)


def spatial_attention(h, packed):
    frames, tokens, width = h.shape
    lanes = packed.shape[1] // 4
    return pl.pallas_call(
        functools.partial(spatial_kernel, lanes),
        grid=(frames,),
        in_specs=[
            pl.BlockSpec((1, tokens, width), lambda i: (i, 0, 0)),
            pl.BlockSpec(packed.shape, lambda i: (0, 0)),
        ],
        out_specs=pl.BlockSpec((1, tokens, width), lambda i: (i, 0, 0)),
        out_shape=jax.ShapeDtypeStruct((frames, tokens, width), F32),
        compiler_params=pltpu.CompilerParams(vmem_limit_bytes=VMEM_LIMIT),
        cost_estimate=pl.CostEstimate(
            flops=8 * frames * tokens * width * width, bytes_accessed=2 * width * width, transcendentals=0
        ),
    )(h, packed)


def temporal_kernel(lanes, frames, j_ref, w_ref, mod_ref, out_ref):
    ht = layer_norm(j_ref[...].astype(F32), mod_ref[0:1], mod_ref[1:2]).astype(BF16)
    rows = ht.shape[0] // frames
    qkv = jnp.dot(ht, w_ref[...], preferred_element_type=F32).reshape(frames, rows, 4 * lanes)
    query, keys = qkv[:, :, :lanes], qkv[:, :, lanes : 2 * lanes]
    values = qkv[:, :, 2 * lanes : 3 * lanes]
    pairs = (query[:, None] * keys[None]).reshape(frames * frames * rows, lanes)
    gather = (head_of((lanes, 128), 0) == lax.broadcasted_iota(jnp.int32, (lanes, 128), 1)).astype(F32)
    spread = (head_of((128, lanes), 1) == lax.broadcasted_iota(jnp.int32, (128, lanes), 0)).astype(F32)
    scores = jnp.dot(pairs, gather, precision=lax.Precision.HIGHEST, preferred_element_type=F32)
    weights = jnp.exp(scores / math.sqrt(HEAD_DIM)).reshape(frames, frames, rows, 128)
    weights = weights / jnp.sum(weights, axis=1, keepdims=True)
    wide = jnp.dot(
        weights.reshape(frames * frames * rows, 128).astype(BF16),
        spread.astype(BF16),
        preferred_element_type=F32,
    ).reshape(frames, frames, rows, lanes)
    at = jnp.sum(wide * values[None], axis=1).reshape(frames * rows, lanes)
    padded = jnp.concatenate([jnp.zeros((frames * rows, 3 * lanes), F32), at], axis=1).astype(BF16)
    out_ref[...] = lax.dot_general(padded, w_ref[...], NT, preferred_element_type=F32)


def temporal_attention(joined, packed, t_mod, frames):
    rows, width = joined.shape
    return pl.pallas_call(
        functools.partial(temporal_kernel, packed.shape[1] // 4, frames),
        out_shape=jax.ShapeDtypeStruct((rows, width), F32),
        compiler_params=pltpu.CompilerParams(vmem_limit_bytes=VMEM_LIMIT),
        cost_estimate=pl.CostEstimate(
            flops=4 * rows * width * width, bytes_accessed=2 * width * width, transcendentals=0
        ),
    )(joined, packed, t_mod)


def on_device(
    sizes,
    streams,
    modulation,
    s_qkv,
    s_out,
    w_in,
    w_out,
    hint_gain,
    inject_layer,
    hint_weight,
    t_mod,
    t_qkv,
    t_out,
):
    n_groups, n_seq, n_mp, n_branch = (sizes[a] for a in ("groups", "seq", "mp", "branch"))
    group, plane, part, core = (lax.axis_index(a) for a in ("groups", "seq", "mp", "branch"))
    x, mods = streams[0, 0], modulation[0]
    tokens, width = x.shape
    spots = tokens // (n_seq * n_branch * n_mp)
    own_tokens = tokens // n_mp

    def pick(array, index, count, axis):
        size = array.shape[axis] // count
        picked = lax.slice_in_dim(array, 0, size, axis=axis)
        for i in range(1, count):
            picked = jnp.where(index == i, lax.slice_in_dim(array, i * size, (i + 1) * size, axis=axis), picked)
        return picked

    def hop(value, by_group, by_part):
        if by_group % n_groups == 0 and by_part % n_mp == 0:
            return value
        pairs = [
            (g * n_mp + m, (g + by_group) % n_groups * n_mp + (m + by_part) % n_mp)
            for g in range(n_groups)
            for m in range(n_mp)
        ]
        return lax.ppermute(value, ("groups", "mp"), pairs)

    spread = [(g, m) for g in range(n_groups) for m in range(n_mp)]

    def along(value, axis, step):
        count = sizes[axis]
        return lax.ppermute(value, axis, [(i, (i + step) % count) for i in range(count)])

    def after(value, *others):
        return lax.optimization_barrier((value, *others))[0]

    class Ring:
        def __init__(self, piece):
            self.piece = piece
            self.ringed = n_seq == 4
            if self.ringed:
                self.first = (along(piece, "seq", 1), along(piece, "seq", -1))
            else:
                self.first = (lax.all_gather(piece, "seq", axis=0),)

        def whole(self):
            if not self.ringed:
                return self.first[0].reshape(-1, self.piece.shape[1])
            below, above = self.first
            cut = self.piece.shape[0] // 2
            far = jnp.concatenate([along(below[:cut], "seq", 1), along(above[cut:], "seq", -1)], axis=0)
            full = jnp.zeros((n_seq, *self.piece.shape), self.piece.dtype)
            for value, step in ((self.piece, 0), (below, n_seq - 1), (above, 1), (far, 2)):
                full = lax.dynamic_update_index_in_dim(full, value, (plane + step) % n_seq, 0)
            return full.reshape(-1, self.piece.shape[1])

    def share(value, axis, index, dim):
        if sizes[axis] != 2:
            return lax.all_gather(value, axis, axis=dim, tiled=True)
        other = along(value, axis, 1)
        return jnp.where(
            index == 0, jnp.concatenate([value, other], axis=dim), jnp.concatenate([other, value], axis=dim)
        )

    def pack(qkv, out):
        cols = pick(qkv, group, n_groups, 2)
        return jnp.concatenate([cols[:, 0], cols[:, 1], cols[:, 2], pick(out, group, n_groups, 0).T], axis=1)

    def both_cores(piece, rows):
        joined = share(piece.reshape(n_seq, 1, rows, piece.shape[1]), "branch", core, 1)
        return joined.reshape(n_seq * n_branch * rows, piece.shape[1])

    s_ring = Ring(pack(s_qkv[0], s_out[0]))
    up_ring = Ring(pick(w_in[0], group, n_groups, 1))
    down_ring = Ring(after(pick(w_out[0], group, n_groups, 0).T, *s_ring.first))
    hint_piece = pick(hint_weight, core, n_branch, 0)
    hint_ring = Ring(after(hint_piece, *up_ring.first))
    t_piece = pick(pack(t_qkv, t_out), core, n_branch, 0)
    t_ring = Ring(after(t_piece, *down_ring.first))

    s_packed = s_ring.whole()
    up_w = up_ring.whole()
    down_w = down_ring.whole()
    hint_w = both_cores(share(hint_ring.whole(), "mp", part, 1), hint_piece.shape[0])
    t_packed = both_cores(t_ring.whole(), t_piece.shape[0])

    blocks = x.reshape(n_seq * n_branch, n_mp, spots, width)
    x = jnp.concatenate(
        [
            lax.dynamic_index_in_dim(blocks, (part + i) % n_mp, 1, False).reshape(own_tokens, width)
            for i in range(n_mp)
        ],
        axis=0,
    )
    h = layer_norm(x, mods[0], mods[1]).astype(BF16)
    h = jnp.stack([hop(h, -g, 0) for g in range(n_groups)])
    partial_out = spatial_attention(h, s_packed).reshape(n_groups, n_mp, own_tokens, width)

    def sum_at_owner(values):
        total = values[0, 0].astype(F32)
        for g, m in spread[1:]:
            total = total + hop(values[g, m].astype(BF16), g, m).astype(F32)
        return total

    x1 = x[:own_tokens] + mods[2] * sum_at_owner({k: partial_out[k] for k in spread})
    h2 = layer_norm(x1, mods[3], mods[4]).astype(BF16)
    rows = jnp.concatenate([hop(h2, -g, -m) for g, m in spread], axis=0)
    hidden = jax.nn.gelu(jnp.dot(rows, up_w, preferred_element_type=F32), approximate=True).astype(BF16)
    hidden = lax.optimization_barrier(hidden)
    down = lax.dot_general(hidden, down_w, NT, preferred_element_type=F32)
    down = down.reshape(len(spread), own_tokens, width)
    y = x1 + mods[5] * sum_at_owner({k: down[i] for i, k in enumerate(spread)})

    moved = lax.all_to_all(
        y.astype(BF16).reshape(1, n_seq, n_branch, spots, width), "branch", split_axis=2, concat_axis=0, tiled=True
    ).reshape(2, n_seq * spots, width)
    layer = lax.dynamic_index_in_dim(inject_layer, plane, 0, False)
    gain = lax.dynamic_index_in_dim(hint_gain, layer, 0, False)
    hint_in = (moved[0].astype(F32) * gain).astype(BF16)
    joined = moved[1].astype(F32) + jnp.dot(hint_in, hint_w, preferred_element_type=F32)

    joined = lax.all_to_all(
        joined.astype(BF16).reshape(n_seq, spots, width), "seq", split_axis=0, concat_axis=0, tiled=True
    )
    around = jnp.stack([hop(joined, -g, -m) for g, m in spread]).reshape(n_groups, n_mp, n_seq, spots, width)
    order = [(i - part + n_mp) % n_mp for i in range(n_mp)]
    around = jnp.stack([lax.dynamic_index_in_dim(around, i, 1, False) for i in order], axis=1)
    at_in = around.transpose(2, 0, 1, 3, 4)
    partial_t = temporal_attention(at_in.reshape(-1, width), t_packed, t_mod, n_seq)
    partial_t = partial_t.reshape(n_seq, n_groups, n_mp * spots, n_mp, width // n_mp)
    sends = {
        (g, m): lax.dynamic_index_in_dim(partial_t[:, g], (part + m) % n_mp, 2, False)
        for g, m in spread
    }
    result = sum_at_owner(sends)
    mine = around[0].transpose(1, 0, 2, 3).reshape(n_seq, n_mp * spots, n_mp, width // n_mp)
    mine = lax.dynamic_index_in_dim(mine, part, 2, False).astype(F32)
    gate = lax.dynamic_index_in_dim(t_mod[2].reshape(n_mp, width // n_mp), part, 0, False)
    return mine + gate * result


def solution(mesh):
    in_specs = (
        P("branch", ("groups", "seq"), None, None),
        P("branch", None, None),
        P("branch", "seq", None, "mp"),
        P("branch", "mp", "seq"),
        P("branch", "seq", "mp"),
        P("branch", "mp", "seq"),
        P(),
        P(),
        P("seq", "mp"),
        P(),
        P("seq", None, "mp"),
        P("mp", "seq"),
    )
    out_specs = P("groups", ("seq", "branch"), "mp")
    return jax.shard_map(
        functools.partial(on_device, dict(mesh.shape)),
        mesh=mesh,
        in_specs=in_specs,
        out_specs=out_specs,
        check_vma=False,
    )
```
